32 devices in a mesh: leaf: 4 (over y, core), panel: 8 (over z, x).
Axes of the slice: x: 2, y: 2, z: 4, core: 2. Of those that a mesh axis runs over, the one named last changes fastest.
Arguments:
- pivot_rhs: float32 [4, 48, 4096], P('leaf', None, 'panel'), may hold values from -6 to 6
- subtree_update: float32 [4, 64, 4096], P('leaf', None, 'panel'), may hold values from -6 to 6
- lower_pivot: bfloat16 [2, 4, 4096, 4096], P(None, 'leaf', 'panel'), as said below
- lower_update: bfloat16 [2, 4, 4096, 4096], P(None, 'leaf', None, 'panel'), as said below
- row_map: int32 [2, 4, 2, 4096], P(None, 'leaf', None, 'panel'), may hold values from 0 to 1023, as said below
- root_inverse: bfloat16 [4096, 4096], P('panel'), as said below
Outputs:
- pivot_solution: float32 [4, 48, 4096], P('leaf', None, 'panel')
- subtree_solution: float32 [4, 64, 4096], P('leaf', None, 'panel')
The draws below stay inside these ranges and needn't reach their ends.
Inputs may be any that keep to these rules, and one draw needn't show every extreme that they name: row_map[l, i] is the same for all i that share i >> (l + 1); within one panel block of 512 rows of one child the values are distinct. lower_pivot[l, i] is the same for all i that share i >> (l + 1), and is zero above its diagonal blocks of 512 rows. lower_update[l, i] is the same for all i that share i >> (l + 1). root_inverse is symmetric.
All inputs are finite; a program needn't handle non-finite values.
Results may differ from the reference program's by a relative error of at most 0.0003.
Values sent between devices are 32-bit elements; how exact they have to be, the bound alone decides.
A program may use at most 64 MiB of HBM per device.

```python
import math
import jax
import jax.numpy as jnp
from jax import lax

VECS = 64
PIV = 4096
UPD = 4096
LEVELS = 2
PBLK = 512
UBLK = 512
OUTCOLS = 48
N_LEAF = 4
N_PANEL = 8


def draw_noise(key, shape):
    return jax.random.normal(key, shape, jnp.float32)


def draw_lower_pivot(key, part):
    block_ids = jnp.arange(PIV) // PBLK
    below_diag = block_ids[:, None] > block_ids[None, :]
    same_block = block_ids[:, None] == block_ids[None, :]
    per_level = []
    for tree_level in range(LEVELS):
        repeat_count = 2 ** (tree_level + 1)
        front_count = N_LEAF // repeat_count
        key_strict, key_inner = jax.random.split(jax.random.fold_in(key, 11 + tree_level))
        strict_part = draw_noise(key_strict, (front_count, PIV, PIV)) * (0.5 / math.sqrt(PIV))
        inner_part = draw_noise(key_inner, (front_count, PIV, PIV)) * (0.3 / math.sqrt(PBLK)) + 0.8 * jnp.eye(PIV, dtype=jnp.float32)
        whole_block = jnp.where(below_diag, strict_part, jnp.where(same_block, inner_part, 0.0)).astype(jnp.bfloat16)
        per_level.append(jnp.repeat(whole_block, repeat_count, axis=0))
    return jnp.stack(per_level)


def draw_lower_update(key, part):
    per_level = []
    for tree_level in range(LEVELS):
        repeat_count = 2 ** (tree_level + 1)
        front_count = N_LEAF // repeat_count
        values = draw_noise(jax.random.fold_in(key, 21 + tree_level), (front_count, UPD, PIV)) * (0.5 / math.sqrt(PIV))
        per_level.append(jnp.repeat(values.astype(jnp.bfloat16), repeat_count, axis=0))
    return jnp.stack(per_level)


def draw_row_map(key, part):
    slot_count = PBLK + UBLK
    per_level = []
    for tree_level in range(LEVELS):
        repeat_count = 2 ** (tree_level + 1)
        front_count = N_LEAF // repeat_count
        scores = jax.random.randint(jax.random.fold_in(key, 31 + tree_level), (front_count, 2, N_PANEL, slot_count), 0, 2 ** 19, dtype=jnp.int32)
        scores = scores * 2048 + jnp.arange(slot_count, dtype=jnp.int32)
        chosen = jnp.argsort(scores, axis=-1)[..., :UBLK].astype(jnp.int32)
        chosen = chosen.reshape(front_count, 2, UPD)
        per_level.append(jnp.repeat(chosen, repeat_count, axis=0))
    return jnp.stack(per_level)


def draw_root_inverse(key, part):
    base_values = draw_noise(key, (UPD, UPD)) * (0.8 / math.sqrt(UPD))
    symmetric = 0.5 * (base_values + base_values.T) + 0.8 * jnp.eye(UPD, dtype=jnp.float32)
    return symmetric.astype(jnp.bfloat16)


def level_of(rng, dims, cuts, least, high):
    level = 1.0
    for axis_at, shards_of in cuts:
        draws = jax.random.uniform(jax.random.fold_in(jax.random.fold_in(rng, 6), axis_at), (shards_of,), jnp.float32, least / len(cuts), high / len(cuts))
        level = level * jnp.repeat(jnp.exp(draws), dims[axis_at] // shards_of).reshape((-1,) + (1,) * (len(dims) - 1 - axis_at))
    return level


def noise(own_key, shape, width, limit, shards=(), kind=jnp.bfloat16):
    drawn = width * jax.random.normal(own_key, shape, jnp.float32)
    if shards:
        drawn = drawn * level_of(own_key, shape, shards, -0.22, 0.18)
    return jnp.clip(drawn, -limit, limit).astype(kind)


def setup_inputs(seed: int = 0) -> dict:
    splits = jax.random.split(jax.random.key(seed), 7)
    return {
        "pivot_rhs": noise(splits[0], (N_LEAF, OUTCOLS, PIV), 1.0, 6.0, ((0, 4), (2, 8)), jnp.float32),
        "subtree_update": noise(splits[1], (N_LEAF, VECS, UPD), 1.0, 6.0, ((0, 4), (2, 8)), jnp.float32),
        "lower_pivot": draw_lower_pivot(jax.random.fold_in(splits[6], 71), 0),
        "lower_update": draw_lower_update(jax.random.fold_in(splits[6], 71), 0),
        "row_map": draw_row_map(jax.random.fold_in(splits[6], 71), 0),
        "root_inverse": draw_root_inverse(jax.random.fold_in(splits[6], 71), 0),
    }


HIGHEST_PRECISION = lax.Precision.HIGHEST


def front_rhs(pivot_rhs, tree_level):
    spread = 2 ** tree_level
    col_count = VECS // spread
    offset = VECS - 2 * col_count
    piece = pivot_rhs[:, offset:offset + col_count, :].reshape(N_LEAF // spread, spread, col_count, PIV)
    return jnp.transpose(piece, (0, 2, 1, 3)).reshape(N_LEAF // spread, VECS, PIV)


def leaf_layout(solution, tree_level):
    spread = 2 ** tree_level
    col_count = VECS // spread
    piece = solution.reshape(N_LEAF // spread, col_count, spread, PIV)
    return jnp.transpose(piece, (0, 2, 1, 3)).reshape(N_LEAF, col_count, PIV)


def front_targets(maps):
    block_ids = (jnp.arange(UPD) // UBLK).astype(jnp.int32)
    pivot_target = block_ids * PBLK + maps
    update_target = PIV + block_ids * UBLK + maps - PBLK
    return jnp.where(maps < PBLK, pivot_target, update_target).astype(jnp.int32)


def assemble_front(kid_values, kid_rows):
    front_sum = jnp.zeros((VECS, PIV + UPD), jnp.float32)
    front_sum = front_sum.at[:, kid_rows[0]].add(kid_values[0])
    return front_sum.at[:, kid_rows[1]].add(kid_values[1])


def pick_front(front_values, kid_rows):
    return jnp.stack([front_values[:, kid_rows[0]], front_values[:, kid_rows[1]]])


def reference(pivot_rhs, subtree_update, lower_pivot, lower_update, row_map, root_inverse):
    solved_levels = []
    reduced = subtree_update
    for tree_level in range(1, LEVELS + 1):
        spread = 2 ** tree_level
        front_count = N_LEAF // spread
        pivot_factor = lower_pivot[tree_level - 1, ::spread].astype(jnp.float32)
        update_factor = lower_update[tree_level - 1, ::spread].astype(jnp.float32)
        targets = front_targets(row_map[tree_level - 1, ::spread])
        assembled = jax.vmap(assemble_front)(reduced.reshape(front_count, 2, VECS, UPD), targets)
        right_side = front_rhs(pivot_rhs, tree_level) + assembled[:, :, :PIV]
        solution = jnp.einsum("fip,fvp->fvi", pivot_factor, right_side, precision=HIGHEST_PRECISION)
        solved_levels.append(solution)
        reduced = assembled[:, :, PIV:] - jnp.einsum("frp,fvp->fvr", update_factor, solution, precision=HIGHEST_PRECISION)
    root_values = jnp.dot(reduced[0], root_inverse.astype(jnp.float32).T, precision=HIGHEST_PRECISION)
    known = root_values[None]
    pieces = [None] * LEVELS
    for tree_level in range(LEVELS, 0, -1):
        spread = 2 ** tree_level
        front_count = N_LEAF // spread
        pivot_factor = lower_pivot[tree_level - 1, ::spread].astype(jnp.float32)
        update_factor = lower_update[tree_level - 1, ::spread].astype(jnp.float32)
        targets = front_targets(row_map[tree_level - 1, ::spread])
        coupling = jnp.einsum("frp,fvr->fvp", update_factor, known, precision=HIGHEST_PRECISION)
        residual_part = solved_levels[tree_level - 1] - coupling
        solution = jnp.einsum("fip,fvi->fvp", pivot_factor, residual_part, precision=HIGHEST_PRECISION)
        pieces[tree_level - 1] = leaf_layout(solution, tree_level)
        whole_front = jnp.concatenate([solution, known], axis=2)
        known = jax.vmap(pick_front)(whole_front, targets).reshape(2 * front_count, VECS, UPD)
    return jnp.concatenate(pieces, axis=1), known
```

```python
import functools

import jax
import jax.numpy as jnp
from jax import lax
from jax.experimental import pallas as pl
from jax.experimental.pallas import tpu as pltpu
from jax.sharding import PartitionSpec as P

MESH = pl.DeviceIdType.MESH
OUTER_MAX = 4
NT = (((1,), (1,)), ((), ()))
NN = (((1,), (0,)), ((), ()))


def bit_reverse(value, bits):
    out = 0
    for i in range(bits):
        out |= (value >> i & 1) << (bits - 1 - i)
    return out


def split(x):
    high = x.astype(jnp.bfloat16).astype(jnp.float32)
    return jnp.concatenate([high, x - high], 0).astype(jnp.bfloat16)


def fold(x):
    half = x.shape[0] // 2
    return x[:half] + x[half:]


def dot(x, w, dims):
    return lax.dot_general(x, w, dims, preferred_element_type=jnp.float32)


def loop(low, high, step, carry):
    if high - low <= 2:
        for i in range(low, high):
            carry = step(i, carry)
        return carry
    return lax.fori_loop(low, high, step, carry)


def kernel(levels, outer, inner, names, *args):
    ref = dict(zip(names, args))
    pivot_in, update_in, maps = ref["pivot_rhs"], ref["subtree_update"], ref["row_map"]
    pivot_out, update_out = ref["pivot_solution"], ref["subtree_solution"]
    pivots, updates, root = ref["pivots"], ref["updates"], ref["root"]
    panels = outer * inner
    pivot_block, update_block = pivot_in.shape[2], update_in.shape[2]
    vectors = update_in.shape[1]
    slots = pivot_block + update_block
    group = vectors >> levels

    leaf = lax.axis_index("leaf")
    panel = lax.axis_index("panel")
    row, col = panel // inner, panel % inner

    bits = [(leaf >> level) & 1 for level in range(levels)]
    counts = [vectors >> (level + 1) for level in range(levels)]
    offsets = [sum(counts[:level]) for level in range(levels)]

    loads = []
    for level in range(levels):
        loads.append(pltpu.make_async_copy(
            ref["lower_pivot"].at[level, 0], pivots.at[level], ref["load_sem"].at[2 * level]))
        loads.append(pltpu.make_async_copy(
            ref["lower_update"].at[level, 0], updates.at[level], ref["load_sem"].at[2 * level + 1]))
    loads.append(pltpu.make_async_copy(ref["root_inverse"], root, ref["load_sem"].at[2 * levels]))
    for load in loads:
        load.start()

    barrier = pltpu.get_barrier_semaphore()
    for d in range(1, outer):
        pl.semaphore_signal(barrier, 1, device_id={"panel": (row ^ d) * inner + col}, device_id_type=MESH)
    for e in range(1, inner):
        pl.semaphore_signal(barrier, 1, device_id={"panel": row * inner + (col ^ e)}, device_id_type=MESH)
    for level in range(levels):
        pl.semaphore_signal(barrier, 1, device_id={"leaf": leaf ^ (1 << level)}, device_id_type=MESH)

    first = ref["current0"]
    for g in range(1 << levels):
        for k in range(group):
            first[pl.ds(g * group + k, 1), :] = update_in[0, pl.ds(k << levels | bit_reverse(g, levels), 1), :]
    for level in range(levels):
        size = levels - 1 - level
        for g in range(1 << size):
            for k in range(group):
                ref["rhs%d" % level][pl.ds(g * group + k, 1), :] = pivot_in[
                    0, pl.ds(offsets[level] + (k << size | bit_reverse(g, size)), 1), :]
    pl.semaphore_wait(barrier, outer - 1 + inner - 1 + levels)

    row_order = [d for d in (1, 3, 2) if d < outer]
    far_order = [d for d in (3, 2, 1) if d < outer]

    def place(d, e):
        return (row ^ d) * inner + (col ^ e)

    def send(source, target, which, slot, device):
        return pltpu.make_async_remote_copy(
            src_ref=source, dst_ref=target, send_sem=ref["send_sem"].at[which, slot],
            recv_sem=ref["recv_sem"].at[which, slot], device_id=device, device_id_type=MESH)

    def to_row(source, target, which, slot, d):
        return send(source, target, which, slot, {"panel": (row ^ d) * inner + col})

    def to_col(source, target, which, slot, e):
        return send(source, target, which, slot, {"panel": row * inner + (col ^ e)})

    def gather(which, buf, value, use, acc):
        buf[0] = value
        for d in far_order:
            to_row(buf.at[0], buf.at[d * inner], which, d * inner, d).start()

        def forward(d):
            def go(e, _):
                to_col(buf.at[d * inner], buf.at[d * inner + e], which, d * inner + e, e).start()
                return _
            loop(1, inner, go, 0)

        def arrived(d, acc):
            def go(e, acc):
                slot = d * inner + e
                to_col(buf.at[slot], buf.at[slot], which, slot, e).wait_recv()
                return use(acc, buf[slot], place(d, e))
            return loop(1, inner, go, acc)

        forward(0)
        acc = use(acc, buf[0], place(0, 0))
        last = 0
        for d in row_order:
            to_row(buf.at[d * inner], buf.at[d * inner], which, d * inner, d).wait_recv()
            forward(d)
            acc = use(acc, buf[d * inner], place(d, 0))
            acc = arrived(last, acc)
            last = d
        return arrived(last, acc)

    def scatter(which, part_buf, in_buf, part):
        for d in far_order + [0]:
            def go(e, _, d=d):
                slot = d * inner + e
                part_buf[slot] = part(place(d, e))
                to_col(part_buf.at[slot], in_buf.at[slot], which, slot, e).start()
                return _
            loop(1, inner, go, 0)

        def collect(d):
            def go(e, acc):
                slot = d * inner + e
                to_col(in_buf.at[slot], in_buf.at[slot], which, slot, e).wait_recv()
                return acc + in_buf[slot]
            return loop(1, inner, go, part(place(d, 0)))

        for d in far_order:
            slot = d * inner
            part_buf[slot] = collect(d)
            to_row(part_buf.at[slot], in_buf.at[slot], which, slot, d).start()
        acc = collect(0)
        for d in row_order:
            slot = d * inner
            to_row(in_buf.at[slot], in_buf.at[slot], which, slot, d).wait_recv()
            acc = acc + in_buf[slot]
        return acc

    def swap(source, target, which, level):
        return pltpu.make_async_remote_copy(
            src_ref=source, dst_ref=target, send_sem=ref["swap_send_sem"].at[which],
            recv_sem=ref["swap_recv_sem"].at[which], device_id={"leaf": leaf ^ (1 << level)},
            device_id_type=MESH)

    def block_of(index, size):
        return pl.ds(pl.multiple_of(index * size, size), size)

    swaps = []

    def begin_swap(level):
        count = counts[level]
        copy = swap(ref["current%d" % level].at[block_of(1 - bits[level], count)],
                    ref["swapped%d" % level], level, level)
        copy.start()
        swaps.append(copy)
        return copy

    copy = begin_swap(0)

    chunk = min(128, slots)
    for level in range(levels):
        for side in range(2):
            child = bits[level] if side == 0 else 1 - bits[level]
            target = maps[level, 0, pl.ds(child, 1), :]

            def fill(i, _, level=level, side=side, target=target):
                rows = lax.broadcasted_iota(jnp.int32, (chunk, update_block), 0) + i * chunk
                ref["tables"][level, side, block_of(i, chunk), :] = jnp.where(
                    rows == target, 1.0, 0.0).astype(jnp.bfloat16)
                return _
            lax.fori_loop(0, slots // chunk, fill, 0)

    tables = ref["tables"]
    for level in range(levels):
        count = counts[level]
        current = ref["current%d" % level]
        if level:
            copy = begin_swap(level)
        total = dot(split(current[block_of(bits[level], count), :]), tables[level, 0], NT)
        copy.wait_recv()
        total = total + dot(split(ref["swapped%d" % level][...]), tables[level, 1], NT)
        assembled = fold(total)
        ref["kept%d" % level][...] = assembled[:, pivot_block:]
        loads[2 * level].wait()

        def use(acc, value, index, level=level):
            return acc + dot(split(value), pivots[level, :, block_of(index, pivot_block)], NT)

        solved = fold(gather(2 * level, ref["gather%d" % (2 * level)],
                             ref["rhs%d" % level][...] + assembled[:, :pivot_block], use, jnp.zeros((2 * count, pivot_block), jnp.float32)))
        ref["solved%d" % level][...] = solved
        pair = ref["pair%d" % level]
        pair[...] = split(solved)
        loads[2 * level + 1].wait()

        def part(index, level=level, pair=pair):
            return fold(dot(pair[...], updates[level, block_of(index, update_block), :], NT))

        coupled = scatter(2 * level + 1, ref["part%d" % (2 * level + 1)], ref["land%d" % (2 * level + 1)], part)
        ref["current%d" % (level + 1)][...] = ref["kept%d" % level][...] - coupled

    loads[2 * levels].wait()
    count = counts[levels - 1]

    def use_root(acc, value, index):
        return acc + dot(split(value), root[:, block_of(index, update_block)], NT)

    known = fold(gather(2 * levels, ref["gather%d" % (2 * levels)], ref["current%d" % levels][...],
                        use_root, jnp.zeros((2 * count, update_block), jnp.float32)))
    ref["known%d" % levels][...] = known

    for level in range(levels - 1, -1, -1):
        count = counts[level]
        which = 2 * levels + 1 + 2 * level
        known = ref["known%d" % (level + 1)]

        def use(acc, value, index, level=level):
            return acc + dot(split(value), updates[level, block_of(index, update_block), :], NN)

        coupling = fold(gather(which, ref["gather%d" % which], known[...], use,
                               jnp.zeros((2 * count, pivot_block), jnp.float32)))
        pair = ref["pair%d" % level]
        pair[...] = split(ref["solved%d" % level][...] - coupling)

        def part(index, level=level, pair=pair):
            return fold(dot(pair[...], pivots[level, :, block_of(index, pivot_block)], NN))

        own = scatter(which + 1, ref["part%d" % (which + 1)], ref["land%d" % (which + 1)], part)
        own_pair, known_pair = split(own), split(known[...])

        def child(side):
            return fold(dot(own_pair, tables[level, side, :pivot_block, :], NN)
                        + dot(known_pair, tables[level, side, pivot_block:, :], NN))

        ref["child%d" % level][...] = child(1)
        rows = block_of(bits[level], count)
        copy = swap(ref["child%d" % level], ref["known%d" % level].at[rows], levels + level, level)
        copy.start()
        swaps.append(copy)
        ref["own%d" % level][...] = own
        size = levels - 1 - level
        for g in range(1 << size):
            for k in range(group):
                pivot_out[0, pl.ds(offsets[level] + (k << size | bit_reverse(g, size)), 1), :] = (
                    ref["own%d" % level][pl.ds(g * group + k, 1), :])
        ref["known%d" % level][rows, :] = child(0)
        copy.wait_recv()

    known = ref["known0"]
    for g in range(1 << levels):
        for k in range(group):
            update_out[0, pl.ds(k << levels | bit_reverse(g, levels), 1), :] = known[pl.ds(g * group + k, 1), :]

    for copy in swaps:
        copy.wait_send()
    for which in range(4 * levels + 1):
        if "gather%d" % which in ref:
            buf = ref["gather%d" % which]
        else:
            buf = ref["part%d" % which]

        def finish(slot, _, which=which, buf=buf):
            send(buf.at[slot], buf.at[slot], which, slot, {"panel": panel ^ 1}).wait_send()
            return _
        lax.fori_loop(1, panels, finish, 0)


def local(panels, pivot_rhs, subtree_update, lower_pivot, lower_update, row_map, root_inverse):
    levels = lower_pivot.shape[0]
    pivot_block, update_block = pivot_rhs.shape[2], subtree_update.shape[2]
    vectors = subtree_update.shape[1]
    outer = min(OUTER_MAX, panels)
    inner = panels // outer
    slots = pivot_block + update_block
    f32, bf16 = jnp.float32, jnp.bfloat16
    scratch = {
        "pivots": pltpu.VMEM((levels,) + lower_pivot.shape[2:], bf16),
        "updates": pltpu.VMEM((levels,) + lower_update.shape[2:], bf16),
        "root": pltpu.VMEM(root_inverse.shape, bf16),
        "tables": pltpu.VMEM((levels, 2, slots, update_block), bf16),
    }
    for level in range(levels):
        count = vectors >> (level + 1)
        back = 2 * levels + 1 + 2 * level
        scratch["current%d" % level] = pltpu.VMEM((2 * count, update_block), f32)
        scratch["known%d" % level] = pltpu.VMEM((2 * count, update_block), f32)
        scratch["swapped%d" % level] = pltpu.VMEM((count, update_block), f32)
        scratch["child%d" % level] = pltpu.VMEM((count, update_block), f32)
        scratch["kept%d" % level] = pltpu.VMEM((count, update_block), f32)
        scratch["solved%d" % level] = pltpu.VMEM((count, pivot_block), f32)
        scratch["rhs%d" % level] = pltpu.VMEM((count, pivot_block), f32)
        scratch["own%d" % level] = pltpu.VMEM((count, pivot_block), f32)
        scratch["pair%d" % level] = pltpu.VMEM((2 * count, pivot_block), bf16)
        scratch["gather%d" % (2 * level)] = pltpu.VMEM((panels, count, pivot_block), f32)
        scratch["gather%d" % back] = pltpu.VMEM((panels, count, update_block), f32)
        for which, width in ((2 * level + 1, update_block), (back + 1, pivot_block)):
            scratch["part%d" % which] = pltpu.VMEM((panels, count, width), f32)
            scratch["land%d" % which] = pltpu.VMEM((panels, count, width), f32)
    count = vectors >> levels
    scratch["current%d" % levels] = pltpu.VMEM((count, update_block), f32)
    scratch["known%d" % levels] = pltpu.VMEM((count, update_block), f32)
    scratch["gather%d" % (2 * levels)] = pltpu.VMEM((panels, count, update_block), f32)
    scratch["send_sem"] = pltpu.SemaphoreType.DMA((4 * levels + 1, panels))
    scratch["recv_sem"] = pltpu.SemaphoreType.DMA((4 * levels + 1, panels))
    scratch["swap_send_sem"] = pltpu.SemaphoreType.DMA((2 * levels,))
    scratch["swap_recv_sem"] = pltpu.SemaphoreType.DMA((2 * levels,))
    scratch["load_sem"] = pltpu.SemaphoreType.DMA((2 * levels + 1,))
    names = ["pivot_rhs", "subtree_update", "row_map", "lower_pivot", "lower_update", "root_inverse",
             "pivot_solution", "subtree_solution"] + list(scratch)
    vmem, anywhere = pl.BlockSpec(memory_space=pltpu.VMEM), pl.BlockSpec(memory_space=pl.ANY)
    return pl.pallas_call(
        functools.partial(kernel, levels, outer, inner, names),
        out_shape=(jax.ShapeDtypeStruct(pivot_rhs.shape, f32),
                   jax.ShapeDtypeStruct(subtree_update.shape, f32)),
        in_specs=[vmem] * 3 + [anywhere] * 3,
        out_specs=(vmem, vmem),
        scratch_shapes=list(scratch.values()),
        compiler_params=pltpu.CompilerParams(collective_id=0, has_side_effects=True),
    )(pivot_rhs, subtree_update, row_map, lower_pivot, lower_update, root_inverse)


def solution(mesh):
    in_specs = (
        P("leaf", None, "panel"),
        P("leaf", None, "panel"),
        P(None, "leaf", "panel", None),
        P(None, "leaf", None, "panel"),
        P(None, "leaf", None, "panel"),
        P("panel", None),
    )
    out_specs = (P("leaf", None, "panel"), P("leaf", None, "panel"))
    return jax.shard_map(functools.partial(local, mesh.shape["panel"]), mesh=mesh, in_specs=in_specs,
                         out_specs=out_specs, check_vma=False)
```

```python
import functools

import jax
import jax.numpy as jnp
from jax import lax
from jax.experimental import pallas as pl
from jax.experimental.pallas import tpu as pltpu
from jax.sharding import PartitionSpec as P

MESH = pl.DeviceIdType.MESH
OUTER_MAX = 4
DIRECT_FROM = 1
DIRECT_PANELS = 8
BATCHES = 2
NT = (((1,), (1,)), ((), ()))
NN = (((1,), (0,)), ((), ()))


def bit_reverse(value, bits):
    out = 0
    for i in range(bits):
        out |= (value >> i & 1) << (bits - 1 - i)
    return out


def split(x):
    high = x.astype(jnp.bfloat16).astype(jnp.float32)
    return jnp.concatenate([high, x - high], 0).astype(jnp.bfloat16)


def fold(x):
    half = x.shape[0] // 2
    return x[:half] + x[half:]


def dot(x, w, dims):
    return lax.dot_general(x, w, dims, preferred_element_type=jnp.float32)


def loop(low, high, step, carry):
    if high - low <= 8:
        for i in range(low, high):
            carry = step(i, carry)
        return carry
    return lax.fori_loop(low, high, step, carry)


def kernel(levels, batches, outer, inner, names, *args):
    ref = dict(zip(names, args))
    pivot_in, update_in, maps = ref["pivot_rhs"], ref["subtree_update"], ref["row_map"]
    pivot_out, update_out = ref["pivot_solution"], ref["subtree_solution"]
    pivots, updates, root = ref["pivots"], ref["updates"], ref["root"]
    panels = outer * inner
    pivot_block, update_block = pivot_in.shape[2], update_in.shape[2]
    whole_vectors = update_in.shape[1]
    vectors = whole_vectors // batches
    slots = pivot_block + update_block
    group = vectors >> levels

    leaf = lax.axis_index("leaf")
    panel = lax.axis_index("panel")
    row, col = panel // inner, panel % inner

    bits = [(leaf >> level) & 1 for level in range(levels)]
    counts = [vectors >> (level + 1) for level in range(levels)]
    offsets = [sum(whole_vectors >> (below + 1) for below in range(level)) for level in range(levels)]

    loads = []
    for level in range(levels):
        loads.append(pltpu.make_async_copy(
            ref["lower_pivot"].at[level, 0], pivots.at[level], ref["load_sem"].at[2 * level]))
        loads.append(pltpu.make_async_copy(
            ref["lower_update"].at[level, 0], updates.at[level], ref["load_sem"].at[2 * level + 1]))
    loads.append(pltpu.make_async_copy(ref["root_inverse"], root, ref["load_sem"].at[2 * levels]))
    for load in loads:
        load.start()

    barrier = pltpu.get_barrier_semaphore()
    for d in range(1, outer):
        pl.semaphore_signal(barrier, 1, device_id={"panel": (row ^ d) * inner + col}, device_id_type=MESH)
    for e in range(1, inner):
        pl.semaphore_signal(barrier, 1, device_id={"panel": row * inner + (col ^ e)}, device_id_type=MESH)
    if panels <= DIRECT_PANELS:
        for d in range(1, outer):
            for e in range(1, inner):
                pl.semaphore_signal(
                    barrier, 1, device_id={"panel": (row ^ d) * inner + (col ^ e)}, device_id_type=MESH)
    for level in range(levels):
        pl.semaphore_signal(barrier, 1, device_id={"leaf": leaf ^ (1 << level)}, device_id_type=MESH)

    for batch in range(batches):
        first = ref["current0@%d" % batch]
        for g in range(1 << levels):
            for k in range(group):
                first[pl.ds(g * group + k, 1), :] = update_in[0, pl.ds(batch * vectors + (k << levels | bit_reverse(g, levels)), 1), :]
        for level in range(levels):
            size = levels - 1 - level
            for g in range(1 << size):
                for k in range(group):
                    ref["rhs%d@%d" % (level, batch)][pl.ds(g * group + k, 1), :] = pivot_in[
                        0, pl.ds(offsets[level] + batch * counts[level] + (k << size | bit_reverse(g, size)), 1), :]
    met = panels - 1 if panels <= DIRECT_PANELS else outer - 1 + inner - 1
    pl.semaphore_wait(barrier, met + levels)

    row_order = [d for d in (1, 3, 2) if d < outer]
    far_order = [d for d in (3, 2, 1) if d < outer]

    def place(d, e):
        return (row ^ d) * inner + (col ^ e)

    def send(source, target, which, slot, device):
        batch, which = which
        return pltpu.make_async_remote_copy(
            src_ref=source, dst_ref=target, send_sem=ref["send_sem"].at[batch, which, slot],
            recv_sem=ref["recv_sem"].at[batch, which, slot], device_id=device, device_id_type=MESH)

    def to_row(source, target, which, slot, d):
        return send(source, target, which, slot, {"panel": (row ^ d) * inner + col})

    def to_col(source, target, which, slot, e):
        return send(source, target, which, slot, {"panel": row * inner + (col ^ e)})

    def direct(which):
        which = which[1]
        level = which // 2 if which <= 2 * levels else (which - 2 * levels - 1) // 2
        return level >= DIRECT_FROM and panels <= DIRECT_PANELS

    def to_any(source, target, which, slot, device):
        return send(source, target, which, slot, {"panel": device})

    def gather_direct(which, buf, value, use, acc):
        buf[0] = value

        def go(i, _):
            slot = panels - 1 - i
            to_any(buf.at[0], buf.at[slot], which, slot, place(slot // inner, slot % inner)).start()
            return _
        loop(0, panels - 1, go, 0)
        acc = use(acc, buf[0], place(0, 0))
        yield

        def take(slot, acc):
            index = place(slot // inner, slot % inner)
            to_any(buf.at[slot], buf.at[slot], which, slot, index).wait_recv()
            return use(acc, buf[slot], index)
        return loop(1, panels, take, acc)

    def scatter_direct(which, part_buf, in_buf, part):
        def go(i, _):
            slot = panels - 1 - i
            index = place(slot // inner, slot % inner)
            part_buf[slot] = part(index)
            to_any(part_buf.at[slot], in_buf.at[slot], which, slot, index).start()
            return _
        loop(0, panels - 1, go, 0)
        own = part(place(0, 0))
        yield

        def take(slot, acc):
            index = place(slot // inner, slot % inner)
            to_any(in_buf.at[slot], in_buf.at[slot], which, slot, index).wait_recv()
            return acc + in_buf[slot]
        return loop(1, panels, take, own)

    def gather(which, buf, value, use, acc):
        if direct(which):
            return (yield from gather_direct(which, buf, value, use, acc))
        buf[0] = value
        for d in far_order:
            to_row(buf.at[0], buf.at[d * inner], which, d * inner, d).start()

        def forward(d):
            def go(e, _):
                to_col(buf.at[d * inner], buf.at[d * inner + e], which, d * inner + e, e).start()
                return _
            loop(1, inner, go, 0)

        def arrived(d, acc):
            def go(e, acc):
                slot = d * inner + e
                to_col(buf.at[slot], buf.at[slot], which, slot, e).wait_recv()
                return use(acc, buf[slot], place(d, e))
            return loop(1, inner, go, acc)

        forward(0)
        acc = use(acc, buf[0], place(0, 0))
        yield
        last = 0
        for d in row_order:
            to_row(buf.at[d * inner], buf.at[d * inner], which, d * inner, d).wait_recv()
            forward(d)
            acc = use(acc, buf[d * inner], place(d, 0))
            acc = arrived(last, acc)
            last = d
        yield
        return arrived(last, acc)

    def scatter(which, part_buf, in_buf, part):
        if direct(which):
            return (yield from scatter_direct(which, part_buf, in_buf, part))
        for d in far_order + [0]:
            def go(e, _, d=d):
                slot = d * inner + e
                part_buf[slot] = part(place(d, e))
                to_col(part_buf.at[slot], in_buf.at[slot], which, slot, e).start()
                return _
            loop(1, inner, go, 0)

        yield

        def collect(d):
            def go(e, acc):
                slot = d * inner + e
                to_col(in_buf.at[slot], in_buf.at[slot], which, slot, e).wait_recv()
                return acc + in_buf[slot]
            return loop(1, inner, go, part(place(d, 0)))

        for d in far_order:
            slot = d * inner
            part_buf[slot] = collect(d)
            to_row(part_buf.at[slot], in_buf.at[slot], which, slot, d).start()
        acc = collect(0)
        yield
        for d in row_order:
            slot = d * inner
            to_row(in_buf.at[slot], in_buf.at[slot], which, slot, d).wait_recv()
            acc = acc + in_buf[slot]
        return acc

    def swap(source, target, which, level):
        return pltpu.make_async_remote_copy(
            src_ref=source, dst_ref=target, send_sem=ref["swap_send_sem"].at[which[0], which[1]],
            recv_sem=ref["swap_recv_sem"].at[which[0], which[1]], device_id={"leaf": leaf ^ (1 << level)},
            device_id_type=MESH)

    def block_of(index, size):
        return pl.ds(pl.multiple_of(index * size, size), size)

    swaps = []

    def begin_swap(level, batch):
        count = counts[level]
        copy = swap(ref["current%d@%d" % (level, batch)].at[block_of(1 - bits[level], count)],
                    ref["swapped%d@%d" % (level, batch)], (batch, level), level)
        copy.start()
        swaps.append(copy)
        return copy

    loaded = set()

    def ready(index):
        if index not in loaded:
            loaded.add(index)
            loads[index].wait()

    tables = ref["tables"]

    def run(batch):
        for level in range(levels):
            count = counts[level]
            current = ref["current%d@%d" % (level, batch)]
            copy = begin_swap(level, batch)
            yield
            total = dot(split(current[block_of(bits[level], count), :]), tables[level, 0], NT)
            copy.wait_recv()
            total = total + dot(split(ref["swapped%d@%d" % (level, batch)][...]), tables[level, 1], NT)
            assembled = fold(total)
            ref["kept%d@%d" % (level, batch)][...] = assembled[:, pivot_block:]
            ready(2 * level)

            def use(acc, value, index, level=level):
                return acc + dot(split(value), pivots[level, :, block_of(index, pivot_block)], NT)

            solved = fold((yield from gather((batch, 2 * level), ref["gather%d@%d" % (2 * level, batch)],
                                 ref["rhs%d@%d" % (level, batch)][...] + assembled[:, :pivot_block], use, jnp.zeros((2 * count, pivot_block), jnp.float32))))
            ref["solved%d@%d" % (level, batch)][...] = solved
            pair = ref["pair%d@%d" % (level, batch)]
            pair[...] = split(solved)
            ready(2 * level + 1)

            def part(index, level=level, pair=pair):
                return fold(dot(pair[...], updates[level, block_of(index, update_block), :], NT))

            coupled = yield from scatter((batch, 2 * level + 1), ref["part%d@%d" % (2 * level + 1, batch)], ref["land%d@%d" % (2 * level + 1, batch)], part)
            ref["current%d@%d" % (level + 1, batch)][...] = ref["kept%d@%d" % (level, batch)][...] - coupled

        ready(2 * levels)
        count = counts[levels - 1]

        def use_root(acc, value, index):
            return acc + dot(split(value), root[:, block_of(index, update_block)], NT)

        known = fold((yield from gather((batch, 2 * levels), ref["gather%d@%d" % (2 * levels, batch)], ref["current%d@%d" % (levels, batch)][...],
                            use_root, jnp.zeros((2 * count, update_block), jnp.float32))))
        ref["known%d@%d" % (levels, batch)][...] = known

        for level in range(levels - 1, -1, -1):
            count = counts[level]
            which = 2 * levels + 1 + 2 * level
            known = ref["known%d@%d" % (level + 1, batch)]

            def use(acc, value, index, level=level):
                return acc + dot(split(value), updates[level, block_of(index, update_block), :], NN)

            coupling = fold((yield from gather((batch, which), ref["gather%d@%d" % (which, batch)], known[...], use,
                                   jnp.zeros((2 * count, pivot_block), jnp.float32))))
            pair = ref["pair%d@%d" % (level, batch)]
            pair[...] = split(ref["solved%d@%d" % (level, batch)][...] - coupling)

            def part(index, level=level, pair=pair):
                return fold(dot(pair[...], pivots[level, :, block_of(index, pivot_block)], NN))

            own = yield from scatter((batch, which + 1), ref["part%d@%d" % (which + 1, batch)], ref["land%d@%d" % (which + 1, batch)], part)
            own_pair, known_pair = split(own), split(known[...])

            def child(side):
                return fold(dot(own_pair, tables[level, side, :pivot_block, :], NN)
                            + dot(known_pair, tables[level, side, pivot_block:, :], NN))

            ref["child%d@%d" % (level, batch)][...] = child(1)
            rows = block_of(bits[level], count)
            copy = swap(ref["child%d@%d" % (level, batch)], ref["known%d@%d" % (level, batch)].at[rows], (batch, levels + level), level)
            copy.start()
            swaps.append(copy)
            ref["own%d@%d" % (level, batch)][...] = own
            size = levels - 1 - level
            for g in range(1 << size):
                for k in range(group):
                    pivot_out[0, pl.ds(offsets[level] + batch * count + (k << size | bit_reverse(g, size)), 1), :] = (
                        ref["own%d@%d" % (level, batch)][pl.ds(g * group + k, 1), :])
            ref["known%d@%d" % (level, batch)][rows, :] = child(0)
            yield
            copy.wait_recv()

        known = ref["known0@%d" % batch]
        for g in range(1 << levels):
            for k in range(group):
                update_out[0, pl.ds(batch * vectors + (k << levels | bit_reverse(g, levels)), 1), :] = known[pl.ds(g * group + k, 1), :]

    runs = [run(batch) for batch in range(batches)]
    for one in runs:
        next(one)
    chunk = min(128, slots)
    for level in range(levels):
        for side in range(2):
            child = bits[level] if side == 0 else 1 - bits[level]
            target = maps[level, 0, pl.ds(child, 1), :]

            def fill(i, _, level=level, side=side, target=target):
                rows = lax.broadcasted_iota(jnp.int32, (chunk, update_block), 0) + i * chunk
                ref["tables"][level, side, block_of(i, chunk), :] = jnp.where(
                    rows == target, 1.0, 0.0).astype(jnp.bfloat16)
                return _
            lax.fori_loop(0, slots // chunk, fill, 0)

    while runs:
        runs = [one for one in runs if next(one, True) is None]

    for copy in swaps:
        copy.wait_send()
    for which in range(4 * levels + 1):
        for batch in range(batches):
            name = "gather%d@%d" % (which, batch)
            buf = ref[name] if name in ref else ref["part%d@%d" % (which, batch)]

            def finish(slot, _, which=which, batch=batch, buf=buf):
                send(buf.at[slot], buf.at[slot], (batch, which), slot, {"panel": panel ^ 1}).wait_send()
                return _
            lax.fori_loop(1, panels, finish, 0)


def local(panels, pivot_rhs, subtree_update, lower_pivot, lower_update, row_map, root_inverse):
    levels = lower_pivot.shape[0]
    pivot_block, update_block = pivot_rhs.shape[2], subtree_update.shape[2]
    batches = BATCHES if subtree_update.shape[1] >> levels >= 8 * BATCHES else 1
    vectors = subtree_update.shape[1] // batches
    outer = min(OUTER_MAX, panels)
    inner = panels // outer
    slots = pivot_block + update_block
    f32, bf16 = jnp.float32, jnp.bfloat16
    scratch = {
        "pivots": pltpu.VMEM((levels,) + lower_pivot.shape[2:], bf16),
        "updates": pltpu.VMEM((levels,) + lower_update.shape[2:], bf16),
        "root": pltpu.VMEM(root_inverse.shape, bf16),
        "tables": pltpu.VMEM((levels, 2, slots, update_block), bf16),
    }
    for batch in range(batches):
        for level in range(levels):
            count = vectors >> (level + 1)
            back = 2 * levels + 1 + 2 * level
            scratch["current%d@%d" % (level, batch)] = pltpu.VMEM((2 * count, update_block), f32)
            scratch["known%d@%d" % (level, batch)] = pltpu.VMEM((2 * count, update_block), f32)
            scratch["swapped%d@%d" % (level, batch)] = pltpu.VMEM((count, update_block), f32)
            scratch["child%d@%d" % (level, batch)] = pltpu.VMEM((count, update_block), f32)
            scratch["kept%d@%d" % (level, batch)] = pltpu.VMEM((count, update_block), f32)
            scratch["solved%d@%d" % (level, batch)] = pltpu.VMEM((count, pivot_block), f32)
            scratch["rhs%d@%d" % (level, batch)] = pltpu.VMEM((count, pivot_block), f32)
            scratch["own%d@%d" % (level, batch)] = pltpu.VMEM((count, pivot_block), f32)
            scratch["pair%d@%d" % (level, batch)] = pltpu.VMEM((2 * count, pivot_block), bf16)
            scratch["gather%d@%d" % (2 * level, batch)] = pltpu.VMEM((panels, count, pivot_block), f32)
            scratch["gather%d@%d" % (back, batch)] = pltpu.VMEM((panels, count, update_block), f32)
            for which, width in ((2 * level + 1, update_block), (back + 1, pivot_block)):
                scratch["part%d@%d" % (which, batch)] = pltpu.VMEM((panels, count, width), f32)
                scratch["land%d@%d" % (which, batch)] = pltpu.VMEM((panels, count, width), f32)
        count = vectors >> levels
        scratch["current%d@%d" % (levels, batch)] = pltpu.VMEM((count, update_block), f32)
        scratch["known%d@%d" % (levels, batch)] = pltpu.VMEM((count, update_block), f32)
        scratch["gather%d@%d" % (2 * levels, batch)] = pltpu.VMEM((panels, count, update_block), f32)
    scratch["send_sem"] = pltpu.SemaphoreType.DMA((batches, 4 * levels + 1, panels))
    scratch["recv_sem"] = pltpu.SemaphoreType.DMA((batches, 4 * levels + 1, panels))
    scratch["swap_send_sem"] = pltpu.SemaphoreType.DMA((batches, 2 * levels))
    scratch["swap_recv_sem"] = pltpu.SemaphoreType.DMA((batches, 2 * levels))
    scratch["load_sem"] = pltpu.SemaphoreType.DMA((2 * levels + 1,))
    names = ["pivot_rhs", "subtree_update", "row_map", "lower_pivot", "lower_update", "root_inverse",
             "pivot_solution", "subtree_solution"] + list(scratch)
    vmem, anywhere = pl.BlockSpec(memory_space=pltpu.VMEM), pl.BlockSpec(memory_space=pl.ANY)
    return pl.pallas_call(
        functools.partial(kernel, levels, batches, outer, inner, names),
        out_shape=(jax.ShapeDtypeStruct(pivot_rhs.shape, f32),
                   jax.ShapeDtypeStruct(subtree_update.shape, f32)),
        in_specs=[vmem] * 3 + [anywhere] * 3,
        out_specs=(vmem, vmem),
        scratch_shapes=list(scratch.values()),
        compiler_params=pltpu.CompilerParams(collective_id=0, has_side_effects=True),
    )(pivot_rhs, subtree_update, row_map, lower_pivot, lower_update, root_inverse)


def solution(mesh):
    in_specs = (
        P("leaf", None, "panel"),
        P("leaf", None, "panel"),
        P(None, "leaf", "panel", None),
        P(None, "leaf", None, "panel"),
        P(None, "leaf", None, "panel"),
        P("panel", None),
    )
    out_specs = (P("leaf", None, "panel"), P("leaf", None, "panel"))
    return jax.shard_map(functools.partial(local, mesh.shape["panel"]), mesh=mesh, in_specs=in_specs,
                         out_specs=out_specs, check_vma=False)
```

```python
import functools

import jax
import jax.numpy as jnp
from jax import lax
from jax.experimental import pallas as pl
from jax.experimental.pallas import tpu as pltpu
from jax.sharding import PartitionSpec as P

MESH = pl.DeviceIdType.MESH
OUTER_MAX = 4
DIRECT_FROM = 1
DIRECT_PANELS = 8
BATCHES = 2
NT = (((1,), (1,)), ((), ()))
NN = (((1,), (0,)), ((), ()))


def bit_reverse(value, bits):
    out = 0
    for i in range(bits):
        out |= (value >> i & 1) << (bits - 1 - i)
    return out


def split(x):
    high = x.astype(jnp.bfloat16).astype(jnp.float32)
    return jnp.concatenate([high, x - high], 0).astype(jnp.bfloat16)


def fold(x):
    half = x.shape[0] // 2
    return x[:half] + x[half:]


def dot(x, w, dims):
    return lax.dot_general(x, w, dims, preferred_element_type=jnp.float32)


def loop(low, high, step, carry):
    if high - low <= 8:
        for i in range(low, high):
            carry = step(i, carry)
        return carry
    return lax.fori_loop(low, high, step, carry)


def kernel(levels, batches, outer, inner, names, *args):
    ref = dict(zip(names, args))
    pivot_in, update_in, maps = ref["pivot_rhs"], ref["subtree_update"], ref["row_map"]
    pivot_out, update_out = ref["pivot_solution"], ref["subtree_solution"]
    pivots, updates, root = ref["pivots"], ref["updates"], ref["root"]
    panels = outer * inner
    pivot_block, update_block = pivot_in.shape[2], update_in.shape[2]
    whole_vectors = update_in.shape[1]
    vectors = whole_vectors // batches
    slots = pivot_block + update_block
    group = vectors >> levels

    leaf = lax.axis_index("leaf")
    panel = lax.axis_index("panel")
    row, col = panel // inner, panel % inner

    bits = [(leaf >> level) & 1 for level in range(levels)]
    counts = [vectors >> (level + 1) for level in range(levels)]
    offsets = [sum(whole_vectors >> (below + 1) for below in range(level)) for level in range(levels)]

    loads = []
    for level in range(levels):
        loads.append(pltpu.make_async_copy(
            ref["lower_pivot"].at[level, 0], pivots.at[level], ref["load_sem"].at[2 * level]))
        loads.append(pltpu.make_async_copy(
            ref["lower_update"].at[level, 0], updates.at[level], ref["load_sem"].at[2 * level + 1]))
    loads.append(pltpu.make_async_copy(ref["root_inverse"], root, ref["load_sem"].at[2 * levels]))
    for load in loads:
        load.start()

    barrier = pltpu.get_barrier_semaphore()
    for d in range(1, outer):
        pl.semaphore_signal(barrier, 1, device_id={"panel": (row ^ d) * inner + col}, device_id_type=MESH)
    for e in range(1, inner):
        pl.semaphore_signal(barrier, 1, device_id={"panel": row * inner + (col ^ e)}, device_id_type=MESH)
    if panels <= DIRECT_PANELS:
        for d in range(1, outer):
            for e in range(1, inner):
                pl.semaphore_signal(
                    barrier, 1, device_id={"panel": (row ^ d) * inner + (col ^ e)}, device_id_type=MESH)
    for level in range(levels):
        pl.semaphore_signal(barrier, 1, device_id={"leaf": leaf ^ (1 << level)}, device_id_type=MESH)

    for batch in range(batches):
        first = ref["current0@%d" % batch]
        for g in range(1 << levels):
            for k in range(group):
                first[pl.ds(g * group + k, 1), :] = update_in[0, pl.ds(batch * vectors + (k << levels | bit_reverse(g, levels)), 1), :]
        for level in range(levels):
            size = levels - 1 - level
            for g in range(1 << size):
                for k in range(group):
                    ref["rhs%d@%d" % (level, batch)][pl.ds(g * group + k, 1), :] = pivot_in[
                        0, pl.ds(offsets[level] + batch * counts[level] + (k << size | bit_reverse(g, size)), 1), :]
    met = panels - 1 if panels <= DIRECT_PANELS else outer - 1 + inner - 1
    pl.semaphore_wait(barrier, met + levels)

    row_order = [d for d in (1, 3, 2) if d < outer]
    far_order = [d for d in (3, 2, 1) if d < outer]

    def place(d, e):
        return (row ^ d) * inner + (col ^ e)

    def send(source, target, which, slot, device):
        batch, which = which
        return pltpu.make_async_remote_copy(
            src_ref=source, dst_ref=target, send_sem=ref["send_sem"].at[batch, which, slot],
            recv_sem=ref["recv_sem"].at[batch, which, slot], device_id=device, device_id_type=MESH)

    def to_row(source, target, which, slot, d):
        return send(source, target, which, slot, {"panel": (row ^ d) * inner + col})

    def to_col(source, target, which, slot, e):
        return send(source, target, which, slot, {"panel": row * inner + (col ^ e)})

    def direct(which):
        batch, which = which
        back = which > 2 * levels
        level = (which - 2 * levels - 1) // 2 if back else which // 2
        adds = (which - back) % 2 == 1
        return (level >= DIRECT_FROM or not adds) and panels <= DIRECT_PANELS

    def to_any(source, target, which, slot, device):
        return send(source, target, which, slot, {"panel": device})

    def gather_direct(which, buf, value, use, acc):
        buf[0] = value

        def go(i, _):
            slot = panels - 1 - i
            to_any(buf.at[0], buf.at[slot], which, slot, place(slot // inner, slot % inner)).start()
            return _
        loop(0, panels - 1, go, 0)
        acc = use(acc, buf[0], place(0, 0))
        yield

        def take(slot, acc):
            index = place(slot // inner, slot % inner)
            to_any(buf.at[slot], buf.at[slot], which, slot, index).wait_recv()
            return use(acc, buf[slot], index)
        return loop(1, panels, take, acc)

    def scatter_direct(which, part_buf, in_buf, part):
        def go(i, _):
            slot = panels - 1 - i
            index = place(slot // inner, slot % inner)
            part_buf[slot] = part(index)
            to_any(part_buf.at[slot], in_buf.at[slot], which, slot, index).start()
            return _
        loop(0, panels - 1, go, 0)
        own = part(place(0, 0))
        yield

        def take(slot, acc):
            index = place(slot // inner, slot % inner)
            to_any(in_buf.at[slot], in_buf.at[slot], which, slot, index).wait_recv()
            return acc + in_buf[slot]
        return loop(1, panels, take, own)

    def gather(which, buf, value, use, acc):
        if direct(which):
            return (yield from gather_direct(which, buf, value, use, acc))
        buf[0] = value
        for d in far_order:
            to_row(buf.at[0], buf.at[d * inner], which, d * inner, d).start()

        def forward(d):
            def go(e, _):
                to_col(buf.at[d * inner], buf.at[d * inner + e], which, d * inner + e, e).start()
                return _
            loop(1, inner, go, 0)

        def arrived(d, acc):
            def go(e, acc):
                slot = d * inner + e
                to_col(buf.at[slot], buf.at[slot], which, slot, e).wait_recv()
                return use(acc, buf[slot], place(d, e))
            return loop(1, inner, go, acc)

        forward(0)
        acc = use(acc, buf[0], place(0, 0))
        yield
        last = 0
        for d in row_order:
            to_row(buf.at[d * inner], buf.at[d * inner], which, d * inner, d).wait_recv()
            forward(d)
            acc = use(acc, buf[d * inner], place(d, 0))
            acc = arrived(last, acc)
            last = d
        yield
        return arrived(last, acc)

    def scatter(which, part_buf, in_buf, part):
        if direct(which):
            return (yield from scatter_direct(which, part_buf, in_buf, part))
        for d in far_order + [0]:
            def go(e, _, d=d):
                slot = d * inner + e
                part_buf[slot] = part(place(d, e))
                to_col(part_buf.at[slot], in_buf.at[slot], which, slot, e).start()
                return _
            loop(1, inner, go, 0)

        yield

        def collect(d):
            def go(e, acc):
                slot = d * inner + e
                to_col(in_buf.at[slot], in_buf.at[slot], which, slot, e).wait_recv()
                return acc + in_buf[slot]
            return loop(1, inner, go, part(place(d, 0)))

        for d in far_order:
            slot = d * inner
            part_buf[slot] = collect(d)
            to_row(part_buf.at[slot], in_buf.at[slot], which, slot, d).start()
        acc = collect(0)
        yield
        for d in row_order:
            slot = d * inner
            to_row(in_buf.at[slot], in_buf.at[slot], which, slot, d).wait_recv()
            acc = acc + in_buf[slot]
        return acc

    def swap(source, target, which, level):
        return pltpu.make_async_remote_copy(
            src_ref=source, dst_ref=target, send_sem=ref["swap_send_sem"].at[which[0], which[1]],
            recv_sem=ref["swap_recv_sem"].at[which[0], which[1]], device_id={"leaf": leaf ^ (1 << level)},
            device_id_type=MESH)

    def block_of(index, size):
        return pl.ds(pl.multiple_of(index * size, size), size)

    swaps = []

    def begin_swap(level, batch):
        count = counts[level]
        copy = swap(ref["current%d@%d" % (level, batch)].at[block_of(1 - bits[level], count)],
                    ref["swapped%d@%d" % (level, batch)], (batch, level), level)
        copy.start()
        swaps.append(copy)
        return copy

    loaded = set()

    def ready(index):
        if index not in loaded:
            loaded.add(index)
            loads[index].wait()

    tables = ref["tables"]

    def run(batch):
        for level in range(levels):
            count = counts[level]
            current = ref["current%d@%d" % (level, batch)]
            copy = begin_swap(level, batch)
            yield
            total = dot(split(current[block_of(bits[level], count), :]), tables[level, 0], NT)
            copy.wait_recv()
            total = total + dot(split(ref["swapped%d@%d" % (level, batch)][...]), tables[level, 1], NT)
            assembled = fold(total)
            ref["kept%d@%d" % (level, batch)][...] = assembled[:, pivot_block:]
            ready(2 * level)

            def use(acc, value, index, level=level):
                return acc + dot(split(value), pivots[level, :, block_of(index, pivot_block)], NT)

            solved = fold((yield from gather((batch, 2 * level), ref["gather%d@%d" % (2 * level, batch)],
                                 ref["rhs%d@%d" % (level, batch)][...] + assembled[:, :pivot_block], use, jnp.zeros((2 * count, pivot_block), jnp.float32))))
            ref["solved%d@%d" % (level, batch)][...] = solved
            pair = ref["pair%d@%d" % (level, batch)]
            pair[...] = split(solved)
            ready(2 * level + 1)

            def part(index, level=level, pair=pair):
                return fold(dot(pair[...], updates[level, block_of(index, update_block), :], NT))

            coupled = yield from scatter((batch, 2 * level + 1), ref["part%d@%d" % (2 * level + 1, batch)], ref["land%d@%d" % (2 * level + 1, batch)], part)
            ref["current%d@%d" % (level + 1, batch)][...] = ref["kept%d@%d" % (level, batch)][...] - coupled

        ready(2 * levels)
        count = counts[levels - 1]

        def use_root(acc, value, index):
            return acc + dot(split(value), root[:, block_of(index, update_block)], NT)

        known = fold((yield from gather((batch, 2 * levels), ref["gather%d@%d" % (2 * levels, batch)], ref["current%d@%d" % (levels, batch)][...],
                            use_root, jnp.zeros((2 * count, update_block), jnp.float32))))
        ref["known%d@%d" % (levels, batch)][...] = known

        for level in range(levels - 1, -1, -1):
            count = counts[level]
            which = 2 * levels + 1 + 2 * level
            known = ref["known%d@%d" % (level + 1, batch)]

            def use(acc, value, index, level=level):
                return acc + dot(split(value), updates[level, block_of(index, update_block), :], NN)

            coupling = fold((yield from gather((batch, which), ref["gather%d@%d" % (which, batch)], known[...], use,
                                   jnp.zeros((2 * count, pivot_block), jnp.float32))))
            pair = ref["pair%d@%d" % (level, batch)]
            pair[...] = split(ref["solved%d@%d" % (level, batch)][...] - coupling)

            def part(index, level=level, pair=pair):
                return fold(dot(pair[...], pivots[level, :, block_of(index, pivot_block)], NN))

            own = yield from scatter((batch, which + 1), ref["part%d@%d" % (which + 1, batch)], ref["land%d@%d" % (which + 1, batch)], part)
            own_pair, known_pair = split(own), split(known[...])

            def child(side):
                return fold(dot(own_pair, tables[level, side, :pivot_block, :], NN)
                            + dot(known_pair, tables[level, side, pivot_block:, :], NN))

            ref["child%d@%d" % (level, batch)][...] = child(1)
            rows = block_of(bits[level], count)
            copy = swap(ref["child%d@%d" % (level, batch)], ref["known%d@%d" % (level, batch)].at[rows], (batch, levels + level), level)
            copy.start()
            swaps.append(copy)
            ref["own%d@%d" % (level, batch)][...] = own
            size = levels - 1 - level
            for g in range(1 << size):
                for k in range(group):
                    pivot_out[0, pl.ds(offsets[level] + batch * count + (k << size | bit_reverse(g, size)), 1), :] = (
                        ref["own%d@%d" % (level, batch)][pl.ds(g * group + k, 1), :])
            ref["known%d@%d" % (level, batch)][rows, :] = child(0)
            yield
            copy.wait_recv()

        known = ref["known0@%d" % batch]
        for g in range(1 << levels):
            for k in range(group):
                update_out[0, pl.ds(batch * vectors + (k << levels | bit_reverse(g, levels)), 1), :] = known[pl.ds(g * group + k, 1), :]

    runs = [run(batch) for batch in range(batches)]
    for one in runs:
        next(one)
    chunk = min(128, slots)
    for level in range(levels):
        for side in range(2):
            child = bits[level] if side == 0 else 1 - bits[level]
            target = maps[level, 0, pl.ds(child, 1), :]

            def fill(i, _, level=level, side=side, target=target):
                rows = lax.broadcasted_iota(jnp.int32, (chunk, update_block), 0) + i * chunk
                ref["tables"][level, side, block_of(i, chunk), :] = jnp.where(
                    rows == target, 1.0, 0.0).astype(jnp.bfloat16)
                return _
            lax.fori_loop(0, slots // chunk, fill, 0)

    while runs:
        runs = [one for one in runs if next(one, True) is None]

    for copy in swaps:
        copy.wait_send()
    for which in range(4 * levels + 1):
        for batch in range(batches):
            name = "gather%d@%d" % (which, batch)
            buf = ref[name] if name in ref else ref["part%d@%d" % (which, batch)]

            def finish(slot, _, which=which, batch=batch, buf=buf):
                send(buf.at[slot], buf.at[slot], (batch, which), slot, {"panel": panel ^ 1}).wait_send()
                return _
            lax.fori_loop(1, panels, finish, 0)


def local(panels, pivot_rhs, subtree_update, lower_pivot, lower_update, row_map, root_inverse):
    levels = lower_pivot.shape[0]
    pivot_block, update_block = pivot_rhs.shape[2], subtree_update.shape[2]
    batches = BATCHES if subtree_update.shape[1] >> levels >= 8 * BATCHES else 1
    vectors = subtree_update.shape[1] // batches
    outer = min(OUTER_MAX, panels)
    inner = panels // outer
    slots = pivot_block + update_block
    f32, bf16 = jnp.float32, jnp.bfloat16
    scratch = {
        "pivots": pltpu.VMEM((levels,) + lower_pivot.shape[2:], bf16),
        "updates": pltpu.VMEM((levels,) + lower_update.shape[2:], bf16),
        "root": pltpu.VMEM(root_inverse.shape, bf16),
        "tables": pltpu.VMEM((levels, 2, slots, update_block), bf16),
    }
    for batch in range(batches):
        for level in range(levels):
            count = vectors >> (level + 1)
            back = 2 * levels + 1 + 2 * level
            scratch["current%d@%d" % (level, batch)] = pltpu.VMEM((2 * count, update_block), f32)
            scratch["known%d@%d" % (level, batch)] = pltpu.VMEM((2 * count, update_block), f32)
            scratch["swapped%d@%d" % (level, batch)] = pltpu.VMEM((count, update_block), f32)
            scratch["child%d@%d" % (level, batch)] = pltpu.VMEM((count, update_block), f32)
            scratch["kept%d@%d" % (level, batch)] = pltpu.VMEM((count, update_block), f32)
            scratch["solved%d@%d" % (level, batch)] = pltpu.VMEM((count, pivot_block), f32)
            scratch["rhs%d@%d" % (level, batch)] = pltpu.VMEM((count, pivot_block), f32)
            scratch["own%d@%d" % (level, batch)] = pltpu.VMEM((count, pivot_block), f32)
            scratch["pair%d@%d" % (level, batch)] = pltpu.VMEM((2 * count, pivot_block), bf16)
            scratch["gather%d@%d" % (2 * level, batch)] = pltpu.VMEM((panels, count, pivot_block), f32)
            scratch["gather%d@%d" % (back, batch)] = pltpu.VMEM((panels, count, update_block), f32)
            for which, width in ((2 * level + 1, update_block), (back + 1, pivot_block)):
                scratch["part%d@%d" % (which, batch)] = pltpu.VMEM((panels, count, width), f32)
                scratch["land%d@%d" % (which, batch)] = pltpu.VMEM((panels, count, width), f32)
        count = vectors >> levels
        scratch["current%d@%d" % (levels, batch)] = pltpu.VMEM((count, update_block), f32)
        scratch["known%d@%d" % (levels, batch)] = pltpu.VMEM((count, update_block), f32)
        scratch["gather%d@%d" % (2 * levels, batch)] = pltpu.VMEM((panels, count, update_block), f32)
    scratch["send_sem"] = pltpu.SemaphoreType.DMA((batches, 4 * levels + 1, panels))
    scratch["recv_sem"] = pltpu.SemaphoreType.DMA((batches, 4 * levels + 1, panels))
    scratch["swap_send_sem"] = pltpu.SemaphoreType.DMA((batches, 2 * levels))
    scratch["swap_recv_sem"] = pltpu.SemaphoreType.DMA((batches, 2 * levels))
    scratch["load_sem"] = pltpu.SemaphoreType.DMA((2 * levels + 1,))
    names = ["pivot_rhs", "subtree_update", "row_map", "lower_pivot", "lower_update", "root_inverse",
             "pivot_solution", "subtree_solution"] + list(scratch)
    vmem, anywhere = pl.BlockSpec(memory_space=pltpu.VMEM), pl.BlockSpec(memory_space=pl.ANY)
    return pl.pallas_call(
        functools.partial(kernel, levels, batches, outer, inner, names),
        out_shape=(jax.ShapeDtypeStruct(pivot_rhs.shape, f32),
                   jax.ShapeDtypeStruct(subtree_update.shape, f32)),
        in_specs=[vmem] * 3 + [anywhere] * 3,
        out_specs=(vmem, vmem),
        scratch_shapes=list(scratch.values()),
        compiler_params=pltpu.CompilerParams(collective_id=0, has_side_effects=True),
    )(pivot_rhs, subtree_update, row_map, lower_pivot, lower_update, root_inverse)


def solution(mesh):
    in_specs = (
        P("leaf", None, "panel"),
        P("leaf", None, "panel"),
        P(None, "leaf", "panel", None),
        P(None, "leaf", None, "panel"),
        P(None, "leaf", None, "panel"),
        P("panel", None),
    )
    out_specs = (P("leaf", None, "panel"), P("leaf", None, "panel"))
    return jax.shard_map(functools.partial(local, mesh.shape["panel"]), mesh=mesh, in_specs=in_specs,
                         out_specs=out_specs, check_vma=False)
```
